32 devices in a mesh: trans: 16 (over z, x, core), bin: 2 (over y).
Axes of the slice: x: 2, y: 2, z: 4, core: 2. Of those that a mesh axis runs over, the one named last changes fastest.
Arguments:
- pair_density: bfloat16 [8192, 8000], P('trans', 'bin'), may hold values from -1.5 to 1.5
- bin_index: int32 [8192, 1], P('trans'), may hold values from 0 to 255; in each aligned block of 512 rows (0 to 511, 512 to 1023, ...) at most 4 rows name the same one
- panel_columns: int32 [128], replicated, may hold values from 0 to 7999
Outputs:
- response: float32 [2, 256, 1024000], P(None, None, ('bin', 'trans'))
The draws below stay inside these ranges and needn't reach their ends.
Inputs may be any that keep to these rules, and one draw needn't show every extreme that they name: `bin_index`: among the 512 transitions of one device no bin occurs more than 4 times, and some bin occurs exactly 4 times. `panel_columns`: entries may repeat.
All inputs are finite; a program needn't handle non-finite values.
Results may differ from the reference program's by a relative error of at most 0.0003.
Values may be sent and summed in bfloat16 or wider, within the bound.
No kernel may reach another device: no remote copies, remote signals or barrier semaphores. Data moves between devices by JAX's collectives and lax.ppermute only.
A program may use at most 256 MiB of HBM per device.

```python
import math
import jax
import jax.numpy as jnp
import numpy as np
from jax import lax

G = 8000
PANEL = 128
NB = 256
MOST = 4
TRANS_DEV = 512
TRANS = 8192
N_TRANS = 16
N_BIN = 2


def set_ends(drawn, own_key, least, largest):
    spot = [jax.random.randint(jax.random.fold_in(own_key, axis), (), 0, length) for axis, length in enumerate(drawn.shape)]
    widest = drawn.shape.index(max(drawn.shape))
    beside = spot[:widest] + [(spot[widest] + 1) % drawn.shape[widest]] + spot[widest + 1:]
    return drawn.at[tuple(spot)].set(least).at[tuple(beside)].set(largest)


def levels(stream_key, dims, pieces, smallest, high):
    def one(axis_at, blocks):
        draws = jax.random.uniform(jax.random.fold_in(jax.random.fold_in(stream_key, 6), axis_at), (blocks,), jnp.float32, smallest / len(pieces), high / len(pieces))
        return jnp.repeat(jnp.exp(draws), dims[axis_at] // blocks).reshape((-1,) + (1,) * (len(dims) - axis_at - 1))

    level = one(*pieces[0])
    for cut in pieces[1:]:
        level = level * one(*cut)
    return level


def assign_block(key, own, number, rows, amount, top, limit, lean):
    sequence = jax.random.permutation(key, amount)
    crowded, usual = shares(amount, rows * top, limit, lean, True), shares(amount, rows * top, limit, lean, False)
    places = jnp.arange(amount)

    def named(sizes, turn):
        used = int((sizes > 0).sum())
        fixed = max(1, used // 4)
        passed = fixed + (places - fixed + turn * (used - fixed)) % max(1, amount - fixed)
        return jnp.zeros((amount,), jnp.int32).at[sequence[jnp.where(places < fixed, places, passed)]].set(jnp.asarray(sizes, jnp.int32))

    sizes = jnp.where(number % 4 == 0, named(crowded, number // 4), named(usual, number - number // 4 - 1))
    mixed = jax.random.permutation(jax.random.fold_in(own, 3), amount)
    giver, taker = mixed[0:amount // 2 * 2:2], mixed[1:amount // 2 * 2:2]
    room = jnp.minimum(sizes[giver] - 1, limit - sizes[taker]) // 2
    room = jnp.where((giver == sequence[0]) | (taker == sequence[0]) | (sizes[taker] == 0), 0, jnp.maximum(room, 0))
    passed = jax.random.randint(jax.random.fold_in(own, 4), (amount // 2,), 0, 1 << 20) % (room + 1)
    sizes = sizes.at[giver].add(-passed).at[taker].add(passed)
    members = jnp.searchsorted(jnp.cumsum(sizes), jnp.arange(rows * top), side="right").astype(jnp.int32)
    grid = members.reshape(top, rows).T
    grid = grid[jax.random.permutation(jax.random.fold_in(own, 1), rows)]
    turn = jax.random.randint(jax.random.fold_in(own, 2), (rows, 1), 0, top)
    return jnp.take_along_axis(grid, (jnp.arange(top)[None, :] + turn) % top, axis=1)


def shares(count, total, bound, skew, full):
    weights = [(1 << 20) // math.isqrt(rank ** skew) + 1 for rank in range(1, count + 1)]
    largest = bound if full else min(bound, max(-(-total // count), total * weights[0] // sum(weights)))
    least = 1 if total - largest >= count - 1 else 0
    holding, rest = [largest] + [least] * (count - 1), total - largest - least * (count - 1)
    while rest > 0:
        candidates = [i for i in range(1, count) if holding[i] < largest] or [i for i in range(1, count) if holding[i] < bound]
        pool, budget = sum([weights[i] for i in candidates]), rest
        for i in candidates:
            extra = min(bound - holding[i], max(1, budget * weights[i] // pool), rest)
            holding[i] = holding[i] + extra
            rest = rest - extra
    return np.array(holding)


def bell_draw(rng, shape, deviation, limit, pieces=(), held_as=jnp.bfloat16):
    drawn = deviation * jax.random.normal(rng, shape, jnp.float32)
    if pieces:
        drawn = drawn * levels(rng, shape, pieces, -0.22, 0.18)
    return jnp.clip(drawn, -limit, limit).astype(held_as)


def setup_inputs(seed: int = 0) -> dict:
    arg_keys = jax.random.split(jax.random.key(seed), 4)
    pair_density = bell_draw(arg_keys[0], (TRANS, G), 0.25, 1.5, ((0, 16), (1, 2)))
    bin_index_keys = jax.random.split(jax.random.fold_in(arg_keys[1], 1), TRANS // TRANS_DEV)
    bin_index_turns = jax.random.permutation(jax.random.fold_in(arg_keys[1], 3), TRANS // TRANS_DEV)
    bin_index = jax.vmap(lambda own, number: assign_block(jax.random.fold_in(arg_keys[1], 2), own, number, TRANS_DEV, NB, 1, MOST, 2))(bin_index_keys, bin_index_turns).reshape((TRANS, 1))
    panel_columns = set_ends(jax.random.randint(arg_keys[2], (PANEL,), 0, G), jax.random.fold_in(arg_keys[2], 1), 0, G - 1).astype(jnp.int32)
    return {"pair_density": pair_density, "bin_index": bin_index, "panel_columns": panel_columns}


broaden = 1.5


def kernel_tables():
    freq = jnp.arange(NB, dtype=jnp.int32).astype(jnp.float32) + 0.5
    diff = freq[:, None] - freq[None, :]
    total = freq[:, None] + freq[None, :]
    low = diff * diff + broaden * broaden
    high = total * total + broaden * broaden
    return diff / low - total / high, broaden / high - broaden / low


def reference(pair_density, bin_index, panel_columns):
    bin_number = bin_index[:, 0]
    order = jnp.argsort(bin_number, stable=True)
    counts = jnp.sum((bin_number[:, None] == jnp.arange(NB, dtype=jnp.int32)[None, :]).astype(jnp.int32), axis=0).astype(jnp.int32)
    starts = (jnp.cumsum(counts) - counts).astype(jnp.int32)
    window = N_TRANS * MOST
    panel = pair_density[:, panel_columns]
    rows_sorted = jnp.concatenate([pair_density[order], jnp.zeros((window, G), pair_density.dtype)], axis=0)
    panel_sorted = jnp.concatenate([panel[order], jnp.zeros((window, PANEL), panel.dtype)], axis=0).astype(jnp.float32)
    row_count = G // N_BIN
    kernel_re, kernel_im = kernel_tables()

    def one_block(index):
        rows = lax.dynamic_slice_in_dim(rows_sorted, (index * row_count).astype(jnp.int32), row_count, 1)

        def one_bin(which):
            start = starts[which]
            chosen = lax.dynamic_slice_in_dim(rows, start, window, 0).astype(jnp.float32)
            paired = lax.dynamic_slice_in_dim(panel_sorted, start, window, 0)
            live = (jnp.arange(window, dtype=jnp.int32) < counts[which]).astype(jnp.float32)
            return jnp.dot((chosen * live[:, None]).T, paired, precision=lax.Precision.HIGHEST, preferred_element_type=jnp.float32)

        spectral = lax.map(one_bin, jnp.arange(NB, dtype=jnp.int32))
        flat = spectral.reshape(NB, row_count * PANEL)
        real_part = jnp.dot(kernel_re, flat, precision=lax.Precision.HIGHEST, preferred_element_type=jnp.float32)
        imag_part = jnp.dot(kernel_im, flat, precision=lax.Precision.HIGHEST, preferred_element_type=jnp.float32)
        return jnp.stack([real_part, imag_part])

    blocks = lax.map(one_block, jnp.arange(N_BIN, dtype=jnp.int32))
    return jnp.transpose(blocks, (1, 2, 0, 3)).reshape(2, NB, G * PANEL)
```

```python
import math

import jax
import jax.numpy as jnp
from jax import lax
from jax.experimental import pallas as pl
from jax.experimental.pallas import tpu as pltpu
from jax.sharding import PartitionSpec as P

PANEL = 128
NB = 256
MOST = 4
PAIR = 2
WIN = PAIR * MOST
LANES = 128
UNROLL = 256
GBLOCK = 8

broaden = 1.5


def kernel_tables():
    freq = lax.broadcasted_iota(jnp.int32, (NB,), 0).astype(jnp.float32) + 0.5
    diff = freq[:, None] - freq[None, :]
    total = freq[:, None] + freq[None, :]
    low = diff * diff + broaden * broaden
    high = total * total + broaden * broaden
    return (diff / low - total / high, broaden / high - broaden / low)


def split_tables():
    kernel_re, kernel_im = kernel_tables()
    both = jnp.concatenate([kernel_re, kernel_im], axis=0)
    top = lax.reduce_precision(both, 8, 7)
    rest = (both - top).astype(jnp.bfloat16)
    top = top.astype(jnp.bfloat16)
    return jnp.concatenate([top, rest, top], axis=1)


def windows(row_count, owners):
    piece = row_count * PANEL // owners
    first = [owner * piece // PANEL for owner in range(owners)]
    rows = max(-(-(owner + 1) * piece // PANEL) - first[owner] for owner in range(owners))
    width = -(-max(start % 8 + rows for start in first) // 8) * 8
    begin = lambda owner: jnp.minimum(owner * piece // PANEL // 8 * 8, row_count - width)
    return piece, rows, width, begin


def prepare(pdt, sort, owners, chunk):
    row_count, local_rows = pdt.shape
    piece, rows, width, begin = windows(row_count, owners)
    padded = -(-width // LANES) * LANES

    def body(pdt_ref, sort_ref, out_ref):
        owner = pl.program_id(0)
        shift = owner * piece // PANEL - begin(owner)
        block = lax.dot_general(
            sort_ref[...], pdt_ref[...], (((1,), (1,)), ((), ())), preferred_element_type=jnp.float32
        )
        if padded != width:
            block = jnp.concatenate([block, jnp.zeros((local_rows, padded - width), jnp.float32)], axis=1)
        block = pltpu.roll(block, (padded - shift) % padded, 1)
        out_ref[0] = block[:, chunk * LANES : (chunk + 1) * LANES].astype(jnp.bfloat16)

    return pl.pallas_call(
        body,
        grid=(owners,),
        in_specs=[
            pl.BlockSpec((pl.Element(width), pl.Element(local_rows)), lambda owner: (pl.multiple_of(begin(owner), 8), 0)),
            pl.BlockSpec((local_rows, local_rows), lambda owner: (0, 0)),
        ],
        out_specs=pl.BlockSpec((1, local_rows, LANES), lambda owner: (owner, 0, 0)),
        out_shape=jax.ShapeDtypeStruct((owners, local_rows, LANES), jnp.bfloat16),
        name=f"prepare{chunk}",
    )(pdt, sort)


def unpack(source_ref, wide_ref):
    sources, local_rows, _ = source_ref.shape
    stride = local_rows + WIN

    def one(source, carry):
        wide_ref[pl.ds(source * stride, local_rows), :] = source_ref[source].astype(jnp.float32)
        wide_ref[pl.ds(source * stride + local_rows, WIN), :] = jnp.zeros((WIN, LANES), jnp.float32)
        return carry

    lax.fori_loop(0, sources, one, 0)


def spread_panel(panel, starts):
    sources, local_rows, _ = panel.shape
    stride = local_rows + WIN
    group = max(1, UNROLL // sources)

    def body(starts_ref, panel_ref, out_ref, wide_ref):
        step = pl.program_id(0)

        @pl.when(step == 0)
        def _():
            unpack(panel_ref, wide_ref)

        place = lax.broadcasted_iota(jnp.int32, (WIN, PANEL), 0)

        def one(source, carry):
            for inner in range(group):
                pair = step * group + inner
                base = source * (NB + 1) + pair * PAIR
                edges = [starts_ref[base + k] for k in range(PAIR + 1)]
                found = wide_ref[pl.ds(source * stride + edges[0], WIN), :]
                for k in range(PAIR):
                    live = (place >= edges[k] - edges[0]) & (place < edges[k + 1] - edges[0])
                    out_ref[inner, pl.ds(pl.multiple_of(source * WIN, WIN), WIN), k * PANEL : (k + 1) * PANEL] = jnp.where(
                        live, found, 0.0
                    ).astype(jnp.bfloat16)
            return carry

        lax.fori_loop(0, sources, one, 0)

    pairs = NB // PAIR
    return pl.pallas_call(
        body,
        grid_spec=pltpu.PrefetchScalarGridSpec(
            num_scalar_prefetch=1,
            grid=(pairs // group,),
            in_specs=[pl.BlockSpec(panel.shape, lambda step, starts: (0, 0, 0))],
            out_specs=pl.BlockSpec((group, sources * WIN, PAIR * PANEL), lambda step, starts: (step, 0, 0)),
            scratch_shapes=[pltpu.VMEM((sources * stride, PANEL), jnp.float32)],
        ),
        out_shape=jax.ShapeDtypeStruct((pairs, sources * WIN, PAIR * PANEL), jnp.bfloat16),
        name="spread",
    )(starts.reshape(-1), panel)


def respond(arrived, spread, starts, tables, rows, chunk, before):
    sources, local_rows, _ = arrived.shape
    stride = local_rows + WIN
    pairs = NB // PAIR
    group = max(1, UNROLL // sources)
    lead = pairs // group
    count = min(LANES, rows - chunk * LANES)
    blocks = -(-count // GBLOCK)
    at = chunk * LANES // GBLOCK

    def body(starts_ref, arrived_ref, spread_ref, tables_ref, *rest):
        out_ref, wide_ref, binned_ref = rest[-3:]
        step = pl.program_id(0)

        @pl.when(step == 0)
        def _():
            unpack(arrived_ref, wide_ref)

        @pl.when(step < lead)
        def _():
            for inner in range(group):
                pair = step * group + inner
                parts = []
                for source in range(sources):
                    start = starts_ref[source * (NB + 1) + pair * PAIR]
                    parts.append(wide_ref[pl.ds(source * stride + start, WIN), :].astype(jnp.bfloat16))
                gathered = jnp.concatenate(parts, axis=0)
                binned = lax.dot_general(
                    gathered, spread_ref[inner], (((0,), (0,)), ((), ())), preferred_element_type=jnp.float32
                )
                for k in range(PAIR):
                    binned_ref[pl.ds(pl.multiple_of((pair * PAIR + k) * LANES, LANES), LANES), :] = binned[
                        :, k * PANEL : (k + 1) * PANEL
                    ]

        @pl.when(step >= lead)
        def _():
            for two in range(GBLOCK // 2):
                found = jnp.concatenate(
                    [
                        binned_ref[pl.ds((step - lead) * GBLOCK + two * 2 + k, NB, stride=LANES), :]
                        for k in range(2)
                    ],
                    axis=1,
                )
                top = found.astype(jnp.bfloat16)
                low = (found - top.astype(jnp.float32)).astype(jnp.bfloat16)
                out = jnp.dot(
                    tables_ref[...], jnp.concatenate([top, top, low], axis=0), preferred_element_type=jnp.float32
                )
                out_ref[:, :, two * 2 * PANEL : (two + 1) * 2 * PANEL] = out.reshape(2, NB, 2 * PANEL)

    in_specs = [
        pl.BlockSpec(arrived.shape, lambda step, starts: (0, 0, 0)),
        pl.BlockSpec((group, sources * WIN, PAIR * PANEL), lambda step, starts: (jnp.minimum(step, lead - 1), 0, 0)),
        pl.BlockSpec(tables.shape, lambda step, starts: (0, 0)),
    ]
    args = [starts.reshape(-1), arrived, spread, tables]
    aliases = {}
    if before is not None:
        in_specs.append(pl.BlockSpec(memory_space=pl.ANY))
        aliases = {len(args): 0}
        args.append(before)
    return pl.pallas_call(
        body,
        grid_spec=pltpu.PrefetchScalarGridSpec(
            num_scalar_prefetch=1,
            grid=(lead + blocks,),
            in_specs=in_specs,
            out_specs=pl.BlockSpec(
                (2, NB, GBLOCK * PANEL), lambda step, starts: (0, 0, at + jnp.maximum(step - lead, 0))
            ),
            scratch_shapes=[
                pltpu.VMEM((sources * stride, LANES), jnp.float32),
                pltpu.VMEM((NB * LANES, PANEL), jnp.float32),
            ],
        ),
        out_shape=jax.ShapeDtypeStruct((2, NB, rows * PANEL), jnp.float32),
        input_output_aliases=aliases,
        compiler_params=pltpu.CompilerParams(vmem_limit_bytes=60000 * 1024),
        name=f"respond{chunk}",
    )(*args)


def local(pair_density, bin_index, panel_columns):
    owners = lax.axis_size("trans")
    place = lax.axis_index("trans")
    bin_place = lax.axis_index("bin")
    local_rows, row_count = pair_density.shape
    piece, rows, _, _ = windows(row_count, owners)
    chunks = -(-rows // LANES)
    pdt = pair_density.T
    bins = bin_index[:, 0]
    order = bins * local_rows + lax.broadcasted_iota(jnp.int32, (local_rows,), 0)
    position = jnp.sum((order[:, None] < order[None, :]).astype(jnp.int32), axis=0)
    sort = (lax.broadcasted_iota(jnp.int32, (local_rows, local_rows), 0) == position[None, :]).astype(jnp.bfloat16)

    sends = [prepare(pdt, sort, owners, chunk) for chunk in range(chunks)]
    arrived = [lax.all_to_all(send, "trans", split_axis=0, concat_axis=0, tiled=True) for send in sends]

    selector = (
        panel_columns[:, None] - bin_place * row_count
        == lax.broadcasted_iota(jnp.int32, (PANEL, row_count), 1)
    ).astype(jnp.bfloat16)
    mine = jnp.dot(selector, pdt, preferred_element_type=jnp.float32).astype(jnp.bfloat16)
    mine = lax.dot_general(
        sort, mine, (((1,), (1,)), ((), ())), preferred_element_type=jnp.float32
    ).astype(jnp.bfloat16)
    mine = lax.psum(mine, "bin")
    panel = lax.all_gather(mine, "trans", axis=0)
    every = lax.all_gather(bins, "trans", axis=0)
    starts = jnp.sum(
        (every[:, None, :] < lax.broadcasted_iota(jnp.int32, (1, NB + 1, 1), 1)).astype(jnp.int32), axis=2
    )
    spread = spread_panel(panel, starts)
    tables = split_tables()
    response = None
    for chunk in range(chunks):
        response = respond(arrived[chunk], spread, starts, tables, rows, chunk, response)
    if rows * PANEL != piece:
        response = lax.dynamic_slice_in_dim(response, place * piece % PANEL, piece, 2)
    return response


def solution(mesh):
    placed = (P("trans", "bin"), P("trans", None), P())
    return jax.shard_map(
        local,
        mesh=mesh,
        in_specs=placed,
        out_specs=P(None, None, ("bin", "trans")),
        check_vma=False,
    )
```
